32 devices in a mesh: ia: 4 (over z), ja: 8 (over y, x, core).
Axes of the slice: x: 2, y: 2, z: 4, core: 2. Of those that a mesh axis runs over, the one named last changes fastest.
Arguments:
- pno_basis: bfloat16 [4, 16, 512, 128], P('ia', 'ja'), may hold values from -0.4375 to 0.4375
- domain_map: int32 [4, 16, 512], replicated, may hold values from 0 to 1023, as said below
- amplitudes: float32 [4, 16, 128, 128], P('ia', 'ja'), may hold values from -6 to 6
- exchange_ints: float32 [4, 16, 128, 128], P('ia', 'ja'), may hold values from -6 to 6
- pno_energy: float32 [4, 16, 128], P('ia', 'ja'), may hold values from 0.5 to 3
- row_energy: float32 [4], P('ia'), may hold values from -1.5 to -0.3
- column_energy: float32 [16], P('ja'), may hold values from -1.5 to -0.3
- coupling_rows: float32 [4, 4], P('ia'), may hold values from -0.6 to 0.6
- coupling_columns: float32 [16, 16], P(None, 'ja'), may hold values from -0.6 to 0.6
- row_neighbours: int32 [4, 16, 3], P('ia', 'ja'), may hold values from 0 to 3, as said below
- column_neighbours: int32 [4, 16, 15], P('ia', 'ja'), may hold values from 0 to 15, as said below
- row_counts: int32 [4, 16], P('ia', 'ja'), may hold values from 1 to 3
- column_counts: int32 [4, 16], P('ia', 'ja'), may hold values from 1 to 15
Outputs:
- new_amplitudes: float32 [4, 16, 128, 128], P('ia', 'ja')
- pair_energy: float32 [4, 16], P('ia', 'ja')
The draws below stay inside these ranges and needn't reach their ends.
Inputs may be any that keep to these rules, and one draw needn't show every extreme that they name: `domain_map`: the 512 entries of one pair are distinct. `row_neighbours`: the 3 entries of a pair (i, j) are distinct and differ from i. `column_neighbours`: the 15 entries of a pair (i, j) are distinct and differ from j.
All inputs are finite; a program needn't handle non-finite values.
Results may differ from the reference program's by a relative error of at most 0.008.
Values may be sent and summed in bfloat16 or wider, within the bound.
A program may use at most 64 MiB of HBM per device.

```python
import jax
import jax.numpy as jnp
from jax import lax

NP = 128
NDOM = 512
NVG = 1024
ITERS = 2
NI = 4
NJ = 16
KR = 3
KC = 15


def distinct_picks(key, groups, universe, picked):
    scores = jax.random.randint(key, (groups, universe), 0, 1 << 20) * universe + jnp.arange(universe, dtype=jnp.int32)[None, :]
    return jnp.argsort(scores, axis=1, stable=True)[:, :picked].astype(jnp.int32)


def draw_domain_map(key, part):
    chosen = distinct_picks(jax.random.fold_in(key, 11), NI * NJ, NVG, NDOM)
    return chosen.reshape(NI, NJ, NDOM)


def draw_row_neighbours(key, part):
    chosen = distinct_picks(jax.random.fold_in(key, 12), NI * NJ, NI - 1, KR).reshape(NI, NJ, KR)
    own_rows = jnp.arange(NI, dtype=jnp.int32)[:, None, None]
    return jnp.where(chosen >= own_rows, chosen + 1, chosen)


def draw_column_neighbours(key, part):
    chosen = distinct_picks(jax.random.fold_in(key, 13), NI * NJ, NJ - 1, KC).reshape(NI, NJ, KC)
    own_columns = jnp.arange(NJ, dtype=jnp.int32)[None, :, None]
    return jnp.where(chosen >= own_columns, chosen + 1, chosen)


def plant(values, stream_key, least, top_value):
    longest = values.shape.index(max(values.shape))
    spots = []
    for shift in (0, 1):
        where = [jax.random.randint(jax.random.fold_in(stream_key, axis), (), 0, length) for axis, length in enumerate(values.shape)]
        where[longest] = (where[longest] + shift) % values.shape[longest]
        spots.append(tuple(where))
    return values.at[spots[0]].set(least).at[spots[1]].set(top_value)


def shard_levels(rng, shape, split, least, top_value):
    level = 1.0
    for position, shards_of in split:
        draws = jax.random.uniform(jax.random.fold_in(jax.random.fold_in(rng, 6), position), (shards_of,), jnp.float32, least / len(split), top_value / len(split))
        level = level * jnp.repeat(jnp.exp(draws), shape[position] // shards_of).reshape((-1,) + (1,) * (len(shape) - 1 - position))
    return level


def noise(key, shape, width, limit, pieces=(), held_as=jnp.bfloat16):
    loudness = shard_levels(key, shape, pieces, -0.22, 0.18) if pieces else 1.0
    entries = jax.random.normal(key, shape, jnp.float32) * width * loudness
    return jnp.minimum(jnp.maximum(entries, -limit), limit).astype(held_as)


def setup_inputs(seed: int = 0) -> dict:
    streams_of = jax.random.split(jax.random.key(seed), 14)
    return {
        "pno_basis": noise(streams_of[0], (NI, NJ, NDOM, NP), (NDOM * 35 // 100) ** -0.5, 0.4375, ((0, 4), (1, 8))),
        "domain_map": draw_domain_map(jax.random.fold_in(streams_of[13], 71), 0),
        "amplitudes": noise(streams_of[2], (NI, NJ, NP, NP), 1.0, 6.0, ((0, 4), (1, 8)), jnp.float32),
        "exchange_ints": noise(streams_of[3], (NI, NJ, NP, NP), 1.0, 6.0, ((0, 4), (1, 8)), jnp.float32),
        "pno_energy": jnp.clip(0.5 + 2.5 * jax.random.uniform(streams_of[4], (NI, NJ, NP), jnp.float32) ** shard_levels(streams_of[4], (NI, NJ, NP), ((0, 4), (1, 8)), -0.2, 0.2), 0.5, 3.0),
        "row_energy": jnp.clip(-1.5 + 1.2 * jax.random.uniform(streams_of[5], (NI,), jnp.float32) ** shard_levels(streams_of[5], (NI,), ((0, 4),), -0.2, 0.2), -1.5, -0.3),
        "column_energy": jnp.clip(-1.5 + 1.2 * jax.random.uniform(streams_of[6], (NJ,), jnp.float32) ** shard_levels(streams_of[6], (NJ,), ((0, 8),), -0.2, 0.2), -1.5, -0.3),
        "coupling_rows": jnp.clip(jax.random.uniform(streams_of[7], (NI, NI), jnp.float32, -0.6, 0.6) * shard_levels(streams_of[7], (NI, NI), ((0, 4),), -0.4, 0.0), -0.6, 0.6),
        "coupling_columns": jnp.clip(jax.random.uniform(streams_of[8], (NJ, NJ), jnp.float32, -0.6, 0.6) * shard_levels(streams_of[8], (NJ, NJ), ((1, 8),), -0.4, 0.0), -0.6, 0.6),
        "row_neighbours": draw_row_neighbours(jax.random.fold_in(streams_of[13], 71), 0),
        "column_neighbours": draw_column_neighbours(jax.random.fold_in(streams_of[13], 71), 0),
        "row_counts": plant(jax.random.randint(streams_of[11], (NI, NJ), 1, KR + 1), jax.random.fold_in(streams_of[11], 1), 1, KR).astype(jnp.int32),
        "column_counts": plant(jax.random.randint(streams_of[12], (NI, NJ), 1, KC + 1), jax.random.fold_in(streams_of[12], 1), 1, KC).astype(jnp.int32),
    }


level_shift = 0.3


def embed_basis(domain_entries, basis_block):
    zeroed = jnp.zeros((NVG, basis_block.shape[1]), basis_block.dtype)
    return zeroed.at[domain_entries].set(basis_block)


def reference(pno_basis, domain_map, amplitudes, exchange_ints, pno_energy, row_energy, column_energy, coupling_rows, coupling_columns, row_neighbours, column_neighbours, row_counts, column_counts):
    pair_count = NI * NJ
    flat_basis = pno_basis.reshape(pair_count, NDOM, NP)
    flat_domain = domain_map.reshape(pair_count, NDOM)
    embedded = jax.vmap(embed_basis)(flat_domain, flat_basis)
    row_ids = jnp.arange(NI, dtype=jnp.int32)[:, None, None]
    column_ids = jnp.arange(NJ, dtype=jnp.int32)[None, :, None]
    row_partner = (row_neighbours * NJ + column_ids).reshape(pair_count, KR)
    column_partner = (row_ids * NJ + column_neighbours).reshape(pair_count, KC)
    row_live = jnp.arange(KR, dtype=jnp.int32)[None, None, :] < row_counts[:, :, None]
    column_live = jnp.arange(KC, dtype=jnp.int32)[None, None, :] < column_counts[:, :, None]
    row_weight = jnp.where(row_live, coupling_rows[row_ids, row_neighbours], 0.0).reshape(pair_count, KR)
    column_weight = jnp.where(column_live, coupling_columns[column_neighbours, column_ids], 0.0).reshape(pair_count, KC)
    energy_gap = pno_energy[:, :, :, None] + pno_energy[:, :, None, :] - row_energy[:, None, None, None] - column_energy[None, :, None, None]
    current = amplitudes
    for iteration in range(ITERS):
        rounded = current.astype(jnp.bfloat16).reshape(pair_count, NP, NP)

        def couple_pair(pair_index):
            own_basis = flat_basis[pair_index].astype(jnp.float32)
            own_domain = flat_domain[pair_index]

            def neighbour_term(partner, weight):
                matched = embedded[partner][own_domain].astype(jnp.float32)
                intersection = jnp.dot(own_basis.T, matched).astype(jnp.bfloat16)
                intersection_wide = intersection.astype(jnp.float32)
                halved = jnp.dot(intersection_wide, rounded[partner].astype(jnp.float32)).astype(jnp.bfloat16)
                return weight * jnp.dot(halved.astype(jnp.float32), intersection_wide.T)

            from_rows = jnp.sum(jax.vmap(neighbour_term)(row_partner[pair_index], row_weight[pair_index]), axis=0)
            from_columns = jnp.sum(jax.vmap(neighbour_term)(column_partner[pair_index], column_weight[pair_index]), axis=0)
            return from_rows + from_columns

        coupled = lax.map(couple_pair, jnp.arange(pair_count, dtype=jnp.int32)).reshape(NI, NJ, NP, NP)
        residual = exchange_ints + energy_gap * current - coupled
        current = current - residual / (energy_gap + level_shift)
    pair_energy = jnp.sum(exchange_ints * (2.0 * current - jnp.swapaxes(current, 2, 3)), axis=(2, 3))
    return current, pair_energy
```

```python
import functools

import jax
import jax.numpy as jnp
from jax import lax
from jax.experimental import pallas as pl
from jax.experimental.pallas import tpu as pltpu
from jax.sharding import PartitionSpec as P

ITERS = 2
CORES = 2

level_shift = 0.3


def kernel(
    n_i,
    n_d,
    basis,
    domain,
    amplitudes,
    exchange,
    energy,
    row_energy,
    column_energy,
    coupling_rows,
    coupling_columns,
    row_nbr,
    column_nbr,
    row_cnt,
    column_cnt,
    out,
    pair_out,
    row_bases,
    col_bases,
    row_amps,
    col_amps,
    own_amps,
    basis_t,
    own_dom,
    row_pick,
    col_pick,
    inter,
    half,
    weight,
    plane_send,
    plane_recv,
    mate_send,
    mate_recv,
    up_send,
    up_recv,
    down_send,
    down_recv,
):
    z = lax.axis_index("ia")
    me = lax.axis_index("ja")
    pairs, size, width = basis.shape
    n_j = n_d * pairs
    n_c = n_d // CORES
    core = me % CORES
    chip = me // CORES
    mate = chip * CORES + (CORES - 1 - core)
    chunks = pairs + ITERS

    def chip_at(shift):
        return ((chip + shift + n_c) % n_c) * CORES + core

    def own_piece(c):
        return basis.at[c] if c < pairs else own_amps.at[c - pairs]

    def row_piece(d, c):
        return row_bases.at[d, c] if c < pairs else row_amps.at[c - pairs, d]

    def col_piece(k, c):
        return col_bases.at[k, c] if c < pairs else col_amps.at[c - pairs, k]

    def remote(src, dst, send, recv, device):
        return pltpu.make_async_remote_copy(
            src_ref=src,
            dst_ref=dst,
            send_sem=send,
            recv_sem=recv,
            device_id=device,
            device_id_type=pl.DeviceIdType.MESH,
        )

    def plane(r, c):
        return remote(
            own_piece(c),
            row_piece(me, c),
            plane_send.at[r, c],
            plane_recv.at[r, c],
            (z, chip_at(r)),
        )

    def plane_in(r, c):
        d = chip_at(-r)
        return remote(
            row_piece(d, c), row_piece(d, c), plane_send.at[r, c], plane_recv.at[r, c], (z, d)
        )

    def to_mate(r, c):
        d = chip_at(-r)
        src = own_piece(c) if r == 0 else row_piece(d, c)
        return remote(src, row_piece(d, c), mate_send.at[r, c], mate_recv.at[r, c], (z, mate))

    def mate_source(r):
        return ((chip - r + n_c) % n_c) * CORES + (CORES - 1 - core)

    def mate_in(r, c):
        d = mate_source(r)
        return remote(
            row_piece(d, c), row_piece(d, c), mate_send.at[r, c], mate_recv.at[r, c], (z, mate)
        )

    def lift(t, c, sign):
        k = z - sign * (t - 1)
        src = own_piece(c) if t == 1 else col_piece(k, c)
        send, recv = (up_send, up_recv) if sign > 0 else (down_send, down_recv)
        return remote(src, col_piece(k, c), send.at[t, c], recv.at[t, c], (z + sign, me))

    def lift_in(t, c, sign):
        k = z - sign * t
        send, recv = (up_send, up_recv) if sign > 0 else (down_send, down_recv)
        return remote(
            col_piece(k, c), col_piece(k, c), send.at[t, c], recv.at[t, c], (z - sign, me)
        )

    def has_source(t, sign):
        return z >= t if sign > 0 else z + t <= n_i - 1

    def has_target(sign):
        return z <= n_i - 2 if sign > 0 else z >= 1

    def send_own(c):
        for sign in (1, -1):

            @pl.when(has_target(sign))
            def _():
                lift(1, c, sign).start()

        for r in range(1, n_c):
            plane(r, c).start()
        to_mate(0, c).start()

    def pass_column(t, c):
        for sign in (1, -1):

            @pl.when(has_source(t, sign))
            def _():
                lift_in(t, c, sign).wait_recv()

            if t + 1 < n_i:

                @pl.when(jnp.logical_and(has_source(t, sign), has_target(sign)))
                def _():
                    lift(t + 1, c, sign).start()

    def pass_row(r, c):
        plane_in(r, c).wait_recv()
        to_mate(r, c).start()

    barrier = pltpu.get_barrier_semaphore()

    def greet(device):
        pl.semaphore_signal(
            barrier, inc=1, device_id=device, device_id_type=pl.DeviceIdType.MESH
        )

    greet((z, mate))
    for r in range(1, n_c):
        greet((z, chip_at(r)))
    for sign in (1, -1):

        @pl.when(has_target(sign))
        def _():
            greet((z + sign, me))

    ends = (z + n_i - 1) // n_i + (2 * n_i - 2 - z) // n_i
    pl.semaphore_wait(barrier, n_c + ends)

    for c in range(pairs):
        send_own(c)

    for p in range(pairs):
        own_amps[0, p] = amplitudes[p].astype(jnp.bfloat16)
        basis_t[p] = basis[p].astype(jnp.float32).T.astype(jnp.bfloat16)
        entries = domain[z, pl.ds(me * pairs + p, 1), :]
        own_dom[p] = jnp.broadcast_to(entries, (width, size)).T

    for p in range(pairs):
        slots = column_nbr.shape[1]
        names = lax.broadcasted_iota(jnp.int32, (n_j, slots), 0)
        order = lax.broadcasted_iota(jnp.int32, (n_j, slots), 1)
        hit = jnp.logical_and(column_nbr[p : p + 1, :] == names, order < column_cnt[0, p])
        chosen = jnp.sum(jnp.where(hit, 1.0, 0.0), axis=1, keepdims=True)
        weight[p, 0:n_j, :] = jnp.broadcast_to(
            chosen * coupling_columns[:, p : p + 1], (n_j, width)
        )
        slots = row_nbr.shape[1]
        names = lax.broadcasted_iota(jnp.int32, (n_i, slots), 0)
        order = lax.broadcasted_iota(jnp.int32, (n_i, slots), 1)
        hit = jnp.logical_and(row_nbr[p : p + 1, :] == names, order < row_cnt[0, p])
        chosen = jnp.sum(jnp.where(hit, 1.0, 0.0), axis=1, keepdims=True)
        diagonal = lax.broadcasted_iota(jnp.int32, (n_i, n_i), 0) == lax.broadcasted_iota(
            jnp.int32, (n_i, n_i), 1
        )
        table = jnp.sum(
            jnp.where(diagonal, coupling_rows[...], 0.0), axis=1, keepdims=True
        )
        weight[p, n_j : n_j + n_i, :] = jnp.broadcast_to(chosen * table, (n_i, width))

    def picked(p, entries):
        own = jnp.concatenate([own_dom[p]] * (size // width), axis=1)
        match = jnp.where(own == entries, 1.0, 0.0).astype(jnp.bfloat16)
        return jnp.dot(basis_t[p], match, preferred_element_type=jnp.float32).astype(
            jnp.bfloat16
        )

    def pick_row(q, carry):
        entries = domain[z, pl.ds(q, 1), :]
        for p in range(pairs):
            row_pick[q, p * width : (p + 1) * width, :] = picked(p, entries)
        return carry

    def pick_col(k, carry):
        for p in range(pairs):
            entries = domain[k, pl.ds(me * pairs + p, 1), :]
            col_pick[k, p * width : (p + 1) * width, :] = picked(p, entries)
        return carry

    def lanes(q):
        return pl.ds(pl.multiple_of(q * width, width), width)

    def intersect_row(d, c, bases):
        q = d * pairs + c
        found = jnp.dot(row_pick[q], bases, preferred_element_type=jnp.float32)
        inter[:, lanes(q)] = found.astype(jnp.bfloat16)

    def intersect_col(k, c):
        rows = slice(c * width, (c + 1) * width)
        found = jnp.dot(
            col_pick[k, rows, :], col_bases[k, c], preferred_element_type=jnp.float32
        )
        inter[rows, lanes(n_j + k)] = found.astype(jnp.bfloat16)

    third = n_j // 4
    lax.fori_loop(0, third, pick_row, 0)
    for c in range(pairs):
        send_c = c
        pass_column(1, send_c)
        for r in range(1, n_c):
            pass_row(r, send_c)
        if c == 0:
            send_own(pairs)
        lax.fori_loop((c + 1) * third, (c + 2) * third, pick_row, 0)
    lax.fori_loop((pairs + 1) * third, n_j, pick_row, 0)
    lax.fori_loop(0, n_i, pick_col, 0)

    zero = jnp.zeros((pairs * width, width), jnp.bfloat16)
    inter[:, lanes(n_j + z)] = zero
    half[:, lanes(n_j + z)] = zero
    for c in range(pairs):
        intersect_row(me, c, basis[c])
    for t in range(1, n_i):
        for c in range(pairs):
            if t > 1:
                pass_column(t, c)
            for sign in (1, -1):

                @pl.when(has_source(t, sign))
                def _():
                    intersect_col(z - sign * t, c)

        pass_column(t, pairs)
        if t == 1:
            for r in range(1, n_c):
                pass_row(r, pairs)
            for r in range(1, n_c):
                for c in range(pairs):
                    d = chip_at(-r)
                    intersect_row(d, c, row_bases[d, c])
            for r in range(n_c):
                for c in range(pairs):
                    d = mate_source(r)
                    mate_in(r, c).wait_recv()
                    intersect_row(d, c, row_bases[d, c])
                mate_in(r, pairs).wait_recv()

    def halve_row(it, d, amps):
        for c in range(pairs):
            q = d * pairs + c
            both = jnp.dot(inter[:, lanes(q)], amps[c], preferred_element_type=jnp.float32)
            for p in range(pairs):
                rows = slice(p * width, (p + 1) * width)
                half[rows, lanes(q)] = (both[rows] * weight[p, pl.ds(q, 1), :]).astype(
                    jnp.bfloat16
                )

    def halve_col(it, k):
        for p in range(pairs):
            rows = slice(p * width, (p + 1) * width)
            one = jnp.dot(
                inter[rows, lanes(n_j + k)],
                col_amps[it, k, p],
                preferred_element_type=jnp.float32,
            )
            half[rows, lanes(n_j + k)] = (one * weight[p, pl.ds(n_j + k, 1), :]).astype(
                jnp.bfloat16
            )

    for it in range(ITERS):
        c = pairs + it
        if it > 0:
            send_own(c)
        halve_row(it, me, own_amps.at[it])
        if it > 0:
            pass_column(1, c)
        for r in range(1, n_c):
            if it > 0:
                pass_row(r, c)
        for t in range(1, n_i):
            if it > 0 and t > 1:
                pass_column(t, c)
            if t == 1:
                for r in range(1, n_c):
                    d = chip_at(-r)
                    halve_row(it, d, row_amps.at[it, d])
            for sign in (1, -1):

                @pl.when(has_source(t, sign))
                def _():
                    halve_col(it, z - sign * t)

        for r in range(n_c):
            if it > 0:
                mate_in(r, c).wait_recv()
            d = mate_source(r)
            halve_row(it, d, row_amps.at[it, d])
        for p in range(pairs):
            rows = slice(p * width, (p + 1) * width)
            coupled = lax.dot_general(
                half[rows, :],
                inter[rows, :],
                (((1,), (1,)), ((), ())),
                preferred_element_type=jnp.float32,
            )
            across = jnp.broadcast_to(energy[p : p + 1, :], (width, width))
            gap = across.T + across - row_energy[0] - column_energy[p]
            current = amplitudes[p] if it == 0 else out[p]
            residual = exchange[p] + gap * current - coupled
            current = current - residual / (gap + level_shift)
            out[p] = current
            if it + 1 < ITERS:
                own_amps[it + 1, p] = current.astype(jnp.bfloat16)
            else:
                terms = exchange[p] * (2.0 * current - current.T)
                pair_out[:, p : p + 1] = jnp.sum(
                    jnp.sum(terms, axis=0, keepdims=True), axis=1, keepdims=True
                )

    for c in range(chunks):
        for r in range(1, n_c):
            plane(r, c).wait_send()
        for r in range(n_c):
            to_mate(r, c).wait_send()
        for sign in (1, -1):

            @pl.when(has_target(sign))
            def _():
                lift(1, c, sign).wait_send()

            for t in range(1, n_i - 1):

                @pl.when(jnp.logical_and(has_source(t, sign), has_target(sign)))
                def _():
                    lift(t + 1, c, sign).wait_send()


def local(
    n_i,
    n_d,
    pno_basis,
    domain_map,
    amplitudes,
    exchange_ints,
    pno_energy,
    row_energy,
    column_energy,
    coupling_rows,
    coupling_columns,
    row_neighbours,
    column_neighbours,
    row_counts,
    column_counts,
):
    _, pairs, size, width = pno_basis.shape
    n_j = n_d * pairs
    n_c = n_d // CORES
    chunks = pairs + ITERS
    vmem = pl.BlockSpec(memory_space=pltpu.VMEM)
    smem = pl.BlockSpec(memory_space=pltpu.SMEM)
    bf16 = jnp.bfloat16
    dma = pltpu.SemaphoreType.DMA
    new, pair_energy = pl.pallas_call(
        functools.partial(kernel, n_i, n_d),
        out_shape=(
            jax.ShapeDtypeStruct((pairs, width, width), jnp.float32),
            jax.ShapeDtypeStruct((1, pairs), jnp.float32),
        ),
        in_specs=[vmem] * 5 + [smem] * 2 + [vmem] * 4 + [smem] * 2,
        out_specs=(vmem, vmem),
        scratch_shapes=[
            pltpu.VMEM((n_d, pairs, size, width), bf16),
            pltpu.VMEM((n_i, pairs, size, width), bf16),
            pltpu.VMEM((ITERS, n_d, pairs, width, width), bf16),
            pltpu.VMEM((ITERS, n_i, pairs, width, width), bf16),
            pltpu.VMEM((ITERS, pairs, width, width), bf16),
            pltpu.VMEM((pairs, width, size), bf16),
            pltpu.VMEM((pairs, size, width), jnp.int32),
            pltpu.VMEM((n_j, pairs * width, size), bf16),
            pltpu.VMEM((n_i, pairs * width, size), bf16),
            pltpu.VMEM((pairs * width, (n_j + n_i) * width), bf16),
            pltpu.VMEM((pairs * width, (n_j + n_i) * width), bf16),
            pltpu.VMEM((pairs, n_j + n_i, width), jnp.float32),
            dma((n_c, chunks)),
            dma((n_c, chunks)),
            dma((n_c, chunks)),
            dma((n_c, chunks)),
            dma((n_i, chunks)),
            dma((n_i, chunks)),
            dma((n_i, chunks)),
            dma((n_i, chunks)),
        ],
        compiler_params=pltpu.CompilerParams(collective_id=0, has_side_effects=True),
        name="cepa",
    )(
        pno_basis[0],
        domain_map,
        amplitudes[0],
        exchange_ints[0],
        pno_energy[0],
        row_energy,
        column_energy,
        coupling_rows,
        coupling_columns,
        row_neighbours[0],
        column_neighbours[0],
        row_counts,
        column_counts,
    )
    return new[None], pair_energy


def solution(mesh):
    in_specs = (
        P("ia", "ja", None, None),
        P(),
        P("ia", "ja", None, None),
        P("ia", "ja", None, None),
        P("ia", "ja", None),
        P("ia"),
        P("ja"),
        P("ia", None),
        P(None, "ja"),
        P("ia", "ja", None),
        P("ia", "ja", None),
        P("ia", "ja"),
        P("ia", "ja"),
    )
    out_specs = (P("ia", "ja", None, None), P("ia", "ja"))
    body = functools.partial(local, mesh.shape["ia"], mesh.shape["ja"])
    return jax.shard_map(body, mesh=mesh, in_specs=in_specs, out_specs=out_specs, check_vma=False)
```

```python
import functools

import jax
import jax.numpy as jnp
from jax import lax
from jax.experimental import pallas as pl
from jax.experimental.pallas import tpu as pltpu
from jax.sharding import PartitionSpec as P

ITERS = 2
CORES = 2

level_shift = 0.3


def kernel(
    n_i,
    n_d,
    basis,
    domain,
    amplitudes,
    exchange,
    energy,
    row_energy,
    column_energy,
    coupling_rows,
    coupling_columns,
    row_nbr,
    column_nbr,
    row_cnt,
    column_cnt,
    out,
    pair_out,
    row_bases,
    col_bases,
    row_amps,
    col_amps,
    own_amps,
    basis_t,
    own_dom,
    row_pick,
    col_pick,
    inter,
    half,
    weight,
    back_out,
    back_in,
    plane_send,
    plane_recv,
    mate_send,
    mate_recv,
    up_send,
    up_recv,
    down_send,
    down_recv,
    back_send,
    back_recv,
):
    z = lax.axis_index("ia")
    me = lax.axis_index("ja")
    pairs, size, width = basis.shape
    n_j = n_d * pairs
    n_c = n_d // CORES
    core = me % CORES
    chip = me // CORES
    mate = chip * CORES + (CORES - 1 - core)
    chunks = pairs + ITERS

    side = round(n_c**0.5)
    side = side if side * side == n_c else n_c

    def snake(place):
        line, step = place // side, place % side
        odd = line % 2
        return line * side + step + odd * (side - 1 - 2 * step)

    spot = snake(chip)

    def chip_at(shift):
        return snake((spot + shift + n_c) % n_c) * CORES + core

    relayed = n_c == 4

    def own_piece(c):
        return basis.at[c] if c < pairs else own_amps.at[c - pairs]

    def row_piece(d, c):
        return row_bases.at[d, c] if c < pairs else row_amps.at[c - pairs, d]

    def col_piece(k, c):
        return col_bases.at[k, c] if c < pairs else col_amps.at[c - pairs, k]

    def remote(src, dst, send, recv, device):
        return pltpu.make_async_remote_copy(
            src_ref=src,
            dst_ref=dst,
            send_sem=send,
            recv_sem=recv,
            device_id=device,
            device_id_type=pl.DeviceIdType.MESH,
        )

    def plane(r, c):
        return remote(
            own_piece(c),
            row_piece(me, c),
            plane_send.at[r, c],
            plane_recv.at[r, c],
            (z, chip_at(r)),
        )

    def corner(c):
        way = 1 if c % 2 == 0 else -1
        d = chip_at(-way)
        return remote(
            row_piece(d, c),
            row_piece(d, c),
            plane_send.at[2, c],
            plane_recv.at[2, c],
            (z, chip_at(way)),
        )

    def is_corner(r, c):
        return relayed and r == 2 and c < pairs

    def plane_in(r, c):
        d = chip_at(-r)
        return remote(
            row_piece(d, c), row_piece(d, c), plane_send.at[r, c], plane_recv.at[r, c], (z, d)
        )

    def to_mate(r, c):
        d = chip_at(-r)
        src = own_piece(c) if r == 0 else row_piece(d, c)
        return remote(src, row_piece(d, c), mate_send.at[r, c], mate_recv.at[r, c], (z, mate))

    def mate_source(r):
        return snake((spot - r + n_c) % n_c) * CORES + (CORES - 1 - core)

    def mate_in(r, c):
        d = mate_source(r)
        return remote(
            row_piece(d, c), row_piece(d, c), mate_send.at[r, c], mate_recv.at[r, c], (z, mate)
        )

    def lift(t, c, sign):
        k = z - sign * (t - 1)
        src = own_piece(c) if t == 1 else col_piece(k, c)
        send, recv = (up_send, up_recv) if sign > 0 else (down_send, down_recv)
        return remote(src, col_piece(k, c), send.at[t, c], recv.at[t, c], (z + sign, me))

    def lift_in(t, c, sign):
        k = z - sign * t
        send, recv = (up_send, up_recv) if sign > 0 else (down_send, down_recv)
        return remote(
            col_piece(k, c), col_piece(k, c), send.at[t, c], recv.at[t, c], (z - sign, me)
        )

    def place(sign):
        return z if sign > 0 else n_i - 1 - z

    def is_main(c, sign):
        return (c % 2 == 0) == (sign > 0)

    def both(a, b):
        return jnp.logical_and(a, b)

    def moves(t, c, sign):
        at = place(sign)
        if c >= pairs or (t > 1 and is_main(c, sign)):
            return both(at >= t - 1, at <= n_i - 2)
        if t > 1:
            return None
        return at <= n_i - 3 if is_main(c, sign) else at == 0

    def comes(t, c, sign):
        at = place(sign)
        if c >= pairs or (t > 1 and is_main(c, sign)):
            return at >= t
        if t > 1:
            return None
        return both(at >= 1, at <= n_i - 2) if is_main(c, sign) else at == 1

    def returns(t, c, sign):
        at = place(sign)
        if t == 1:
            return at <= n_i - 3 if is_main(c, sign) else at == 0
        return at <= n_i - 1 - t if is_main(c, sign) else None

    def when(condition, action):
        if condition is not None:
            pl.when(condition)(action)

    def give_back(t, c, sign):
        k = z - sign * t
        spot_of = t + (0 if sign > 0 else n_i)
        return remote(
            back_out.at[k, c],
            back_in.at[z, c],
            back_send.at[spot_of, c],
            back_recv.at[spot_of, c],
            (k, me),
        )

    def take_back(t, c, sign):
        k = z + sign * t
        spot_of = t + (0 if sign > 0 else n_i)
        return remote(
            back_out.at[k, c],
            back_in.at[k, c],
            back_send.at[spot_of, c],
            back_recv.at[spot_of, c],
            (k, me),
        )

    def send_own(c):
        for sign in (1, -1):
            when(moves(1, c, sign), lambda: lift(1, c, sign).start())
        for r in range(1, n_c):
            if not is_corner(r, c):
                plane(r, c).start()
        to_mate(0, c).start()

    def pass_column(t, c):
        for sign in (1, -1):
            arrives = comes(t, c, sign)
            when(arrives, lambda: lift_in(t, c, sign).wait_recv())
            onward = moves(t + 1, c, sign) if t + 1 < n_i else None
            if arrives is not None and onward is not None:
                when(both(arrives, onward), lambda: lift(t + 1, c, sign).start())

    def pass_row(r, c):
        plane_in(r, c).wait_recv()
        if relayed and c < pairs and r == (1 if c % 2 == 0 else n_c - 1):
            corner(c).start()
        to_mate(r, c).start()

    near = [r for r in range(1, n_c) if not is_corner(r, 0)]
    near = near + [r for r in range(1, n_c) if is_corner(r, 0)]

    barrier = pltpu.get_barrier_semaphore()

    def greet(device):
        pl.semaphore_signal(
            barrier, inc=1, device_id=device, device_id_type=pl.DeviceIdType.MESH
        )

    greet((z, mate))
    for r in range(1, n_c):
        greet((z, chip_at(r)))
    for shift in range(1, n_i):
        greet(((z + shift) % n_i, me))
    pl.semaphore_wait(barrier, n_c + n_i - 1)

    for c in range(pairs):
        send_own(c)

    for p in range(pairs):
        own_amps[0, p] = amplitudes[p].astype(jnp.bfloat16)
        basis_t[p] = basis[p].astype(jnp.float32).T.astype(jnp.bfloat16)
        entries = domain[z, pl.ds(me * pairs + p, 1), :]
        own_dom[p] = jnp.broadcast_to(entries, (width, size)).T

    for p in range(pairs):
        slots = column_nbr.shape[1]
        names = lax.broadcasted_iota(jnp.int32, (n_j, slots), 0)
        order = lax.broadcasted_iota(jnp.int32, (n_j, slots), 1)
        hit = jnp.logical_and(column_nbr[p : p + 1, :] == names, order < column_cnt[0, p])
        chosen = jnp.sum(jnp.where(hit, 1.0, 0.0), axis=1, keepdims=True)
        weight[p, 0:n_j, :] = jnp.broadcast_to(
            chosen * coupling_columns[:, p : p + 1], (n_j, width)
        )
        slots = row_nbr.shape[1]
        names = lax.broadcasted_iota(jnp.int32, (n_i, slots), 0)
        order = lax.broadcasted_iota(jnp.int32, (n_i, slots), 1)
        hit = jnp.logical_and(row_nbr[p : p + 1, :] == names, order < row_cnt[0, p])
        chosen = jnp.sum(jnp.where(hit, 1.0, 0.0), axis=1, keepdims=True)
        diagonal = lax.broadcasted_iota(jnp.int32, (n_i, n_i), 0) == lax.broadcasted_iota(
            jnp.int32, (n_i, n_i), 1
        )
        table = jnp.sum(
            jnp.where(diagonal, coupling_rows[...], 0.0), axis=1, keepdims=True
        )
        weight[p, n_j : n_j + n_i, :] = jnp.broadcast_to(chosen * table, (n_i, width))

    def picked(p, entries):
        own = jnp.concatenate([own_dom[p]] * (size // width), axis=1)
        match = jnp.where(own == entries, 1.0, 0.0).astype(jnp.bfloat16)
        return jnp.dot(basis_t[p], match, preferred_element_type=jnp.float32).astype(
            jnp.bfloat16
        )

    def pick_row(q, carry):
        entries = domain[z, pl.ds(q, 1), :]
        for p in range(pairs):
            row_pick[q, p * width : (p + 1) * width, :] = picked(p, entries)
        return carry

    def pick_col(k, carry):
        for p in range(pairs):
            entries = domain[k, pl.ds(me * pairs + p, 1), :]
            col_pick[k, p * width : (p + 1) * width, :] = picked(p, entries)
        return carry

    def lanes(q):
        return pl.ds(pl.multiple_of(q * width, width), width)

    def intersect_row(d, c, bases):
        q = d * pairs + c
        found = jnp.dot(row_pick[q], bases, preferred_element_type=jnp.float32)
        inter[:, lanes(q)] = found.astype(jnp.bfloat16)

    def intersect_col(k, c):
        rows = slice(c * width, (c + 1) * width)
        found = jnp.dot(
            col_pick[k, rows, :], col_bases[k, c], preferred_element_type=jnp.float32
        )
        inter[rows, lanes(n_j + k)] = found.astype(jnp.bfloat16)
        back_out[k, c] = found.astype(jnp.bfloat16)

    def meet_column(t, c):
        for sign in (1, -1):
            when(comes(t, c, sign), lambda: intersect_col(z - sign * t, c))

    def return_column(t, c):
        for sign in (1, -1):
            when(comes(t, c, sign), lambda: give_back(t, c, sign).start())

    def accept_column(t, c):
        rows = slice(c * width, (c + 1) * width)
        for sign in (1, -1):

            def accept():
                take_back(t, c, sign).wait_recv()
                k = z + sign * t
                turned = back_in[k, c].astype(jnp.float32).T
                inter[rows, lanes(n_j + k)] = turned.astype(jnp.bfloat16)

            when(returns(t, c, sign), accept)

    share = n_j // 4
    lax.fori_loop(0, n_i, pick_col, 0)
    send_own(pairs)
    for c in range(pairs):
        pass_column(1, c)
        for r in near:
            if not is_corner(r, c):
                pass_row(r, c)
        meet_column(1, c)
        lax.fori_loop(c * share, (c + 1) * share, pick_row, 0)
        return_column(1, c)
    pass_column(1, pairs)
    zero = jnp.zeros((pairs * width, width), jnp.bfloat16)
    inter[:, lanes(n_j + z)] = zero
    half[:, lanes(n_j + z)] = zero
    for c in range(pairs):
        for r in near:
            if is_corner(r, c):
                pass_row(r, c)
    for t in range(2, n_i):
        for c in range(pairs):
            pass_column(t, c)
            meet_column(t, c)
        if t == 2:
            for r in range(1, n_c):
                pass_row(r, pairs)
            lax.fori_loop(pairs * share, n_j, pick_row, 0)
            for c in range(pairs):
                return_column(t, c)
            for c in range(pairs):
                intersect_row(me, c, basis[c])
        else:
            for c in range(pairs):
                return_column(t, c)
        pass_column(t, pairs)
    for r in near:
        for c in range(pairs):
            d = chip_at(-r)
            intersect_row(d, c, row_bases[d, c])
    for r in range(n_c):
        for c in range(pairs):
            d = mate_source(r)
            mate_in(r, c).wait_recv()
            intersect_row(d, c, row_bases[d, c])
        mate_in(r, pairs).wait_recv()
    for t in range(1, n_i):
        for c in range(pairs):
            accept_column(t, c)

    def halve_row(it, d, amps):
        for c in range(pairs):
            q = d * pairs + c
            pair = jnp.dot(inter[:, lanes(q)], amps[c], preferred_element_type=jnp.float32)
            for p in range(pairs):
                rows = slice(p * width, (p + 1) * width)
                half[rows, lanes(q)] = (pair[rows] * weight[p, pl.ds(q, 1), :]).astype(
                    jnp.bfloat16
                )

    def halve_col(it, k):
        for p in range(pairs):
            rows = slice(p * width, (p + 1) * width)
            one = jnp.dot(
                inter[rows, lanes(n_j + k)],
                col_amps[it, k, p],
                preferred_element_type=jnp.float32,
            )
            half[rows, lanes(n_j + k)] = (one * weight[p, pl.ds(n_j + k, 1), :]).astype(
                jnp.bfloat16
            )

    for it in range(ITERS):
        c = pairs + it
        if it > 0:
            send_own(c)
        halve_row(it, me, own_amps.at[it])
        if it > 0:
            pass_column(1, c)
        for r in range(1, n_c):
            if it > 0:
                pass_row(r, c)
        for t in range(1, n_i):
            if it > 0 and t > 1:
                pass_column(t, c)
            if t == 1:
                for r in range(1, n_c):
                    d = chip_at(-r)
                    halve_row(it, d, row_amps.at[it, d])
            for sign in (1, -1):

                when(comes(t, c, sign), lambda: halve_col(it, z - sign * t))

        for r in range(n_c):
            if it > 0:
                mate_in(r, c).wait_recv()
            d = mate_source(r)
            halve_row(it, d, row_amps.at[it, d])
        for p in range(pairs):
            rows = slice(p * width, (p + 1) * width)
            coupled = lax.dot_general(
                half[rows, :],
                inter[rows, :],
                (((1,), (1,)), ((), ())),
                preferred_element_type=jnp.float32,
            )
            across = jnp.broadcast_to(energy[p : p + 1, :], (width, width))
            gap = across.T + across - row_energy[0] - column_energy[p]
            current = amplitudes[p] if it == 0 else out[p]
            residual = exchange[p] + gap * current - coupled
            current = current - residual / (gap + level_shift)
            out[p] = current
            if it + 1 < ITERS:
                own_amps[it + 1, p] = current.astype(jnp.bfloat16)
            else:
                terms = exchange[p] * (2.0 * current - current.T)
                pair_out[:, p : p + 1] = jnp.sum(
                    jnp.sum(terms, axis=0, keepdims=True), axis=1, keepdims=True
                )

    for c in range(chunks):
        for r in range(1, n_c):
            (corner(c) if is_corner(r, c) else plane(r, c)).wait_send()
        for r in range(n_c):
            to_mate(r, c).wait_send()
        for sign in (1, -1):
            for t in range(1, n_i):
                when(moves(t, c, sign), lambda: lift(t, c, sign).wait_send())
                if c < pairs:
                    when(comes(t, c, sign), lambda: give_back(t, c, sign).wait_send())


def local(
    n_i,
    n_d,
    pno_basis,
    domain_map,
    amplitudes,
    exchange_ints,
    pno_energy,
    row_energy,
    column_energy,
    coupling_rows,
    coupling_columns,
    row_neighbours,
    column_neighbours,
    row_counts,
    column_counts,
):
    _, pairs, size, width = pno_basis.shape
    n_j = n_d * pairs
    n_c = n_d // CORES
    chunks = pairs + ITERS
    vmem = pl.BlockSpec(memory_space=pltpu.VMEM)
    smem = pl.BlockSpec(memory_space=pltpu.SMEM)
    bf16 = jnp.bfloat16
    dma = pltpu.SemaphoreType.DMA
    new, pair_energy = pl.pallas_call(
        functools.partial(kernel, n_i, n_d),
        out_shape=(
            jax.ShapeDtypeStruct((pairs, width, width), jnp.float32),
            jax.ShapeDtypeStruct((1, pairs), jnp.float32),
        ),
        in_specs=[vmem] * 5 + [smem] * 2 + [vmem] * 4 + [smem] * 2,
        out_specs=(vmem, vmem),
        scratch_shapes=[
            pltpu.VMEM((n_d, pairs, size, width), bf16),
            pltpu.VMEM((n_i, pairs, size, width), bf16),
            pltpu.VMEM((ITERS, n_d, pairs, width, width), bf16),
            pltpu.VMEM((ITERS, n_i, pairs, width, width), bf16),
            pltpu.VMEM((ITERS, pairs, width, width), bf16),
            pltpu.VMEM((pairs, width, size), bf16),
            pltpu.VMEM((pairs, size, width), jnp.int32),
            pltpu.VMEM((n_j, pairs * width, size), bf16),
            pltpu.VMEM((n_i, pairs * width, size), bf16),
            pltpu.VMEM((pairs * width, (n_j + n_i) * width), bf16),
            pltpu.VMEM((pairs * width, (n_j + n_i) * width), bf16),
            pltpu.VMEM((pairs, n_j + n_i, width), jnp.float32),
            pltpu.VMEM((n_i, pairs, width, width), bf16),
            pltpu.VMEM((n_i, pairs, width, width), bf16),
            dma((n_c, chunks)),
            dma((n_c, chunks)),
            dma((n_c, chunks)),
            dma((n_c, chunks)),
            dma((n_i, chunks)),
            dma((n_i, chunks)),
            dma((n_i, chunks)),
            dma((n_i, chunks)),
            dma((2 * n_i, pairs)),
            dma((2 * n_i, pairs)),
        ],
        compiler_params=pltpu.CompilerParams(collective_id=0, has_side_effects=True),
        name="cepa",
    )(
        pno_basis[0],
        domain_map,
        amplitudes[0],
        exchange_ints[0],
        pno_energy[0],
        row_energy,
        column_energy,
        coupling_rows,
        coupling_columns,
        row_neighbours[0],
        column_neighbours[0],
        row_counts,
        column_counts,
    )
    return new[None], pair_energy


def solution(mesh):
    in_specs = (
        P("ia", "ja", None, None),
        P(),
        P("ia", "ja", None, None),
        P("ia", "ja", None, None),
        P("ia", "ja", None),
        P("ia"),
        P("ja"),
        P("ia", None),
        P(None, "ja"),
        P("ia", "ja", None),
        P("ia", "ja", None),
        P("ia", "ja"),
        P("ia", "ja"),
    )
    out_specs = (P("ia", "ja", None, None), P("ia", "ja"))
    body = functools.partial(local, mesh.shape["ia"], mesh.shape["ja"])
    return jax.shard_map(body, mesh=mesh, in_specs=in_specs, out_specs=out_specs, check_vma=False)
```

```python
import functools

import jax
import jax.numpy as jnp
from jax import lax
from jax.experimental import pallas as pl
from jax.experimental.pallas import tpu as pltpu
from jax.sharding import PartitionSpec as P

ITERS = 2
CORES = 2
SPLIT = 1

level_shift = 0.3


def kernel(
    n_i,
    n_d,
    basis,
    domain,
    amplitudes,
    exchange,
    energy,
    row_energy,
    column_energy,
    coupling_rows,
    coupling_columns,
    row_nbr,
    column_nbr,
    row_cnt,
    column_cnt,
    out,
    pair_out,
    row_bases,
    col_bases,
    row_amps,
    col_amps,
    own_amps,
    basis_t,
    own_dom,
    row_pick,
    col_pick,
    inter,
    half,
    weight,
    back_out,
    back_in,
    plane_send,
    plane_recv,
    mate_send,
    mate_recv,
    up_send,
    up_recv,
    down_send,
    down_recv,
    back_send,
    back_recv,
):
    z = lax.axis_index("ia")
    me = lax.axis_index("ja")
    pairs, size, width = basis.shape
    n_j = n_d * pairs
    n_c = n_d // CORES
    core = me % CORES
    chip = me // CORES
    mate = chip * CORES + (CORES - 1 - core)
    chunks = pairs + ITERS

    side = round(n_c**0.5)
    side = side if side * side == n_c else n_c

    def snake(place):
        line, step = place // side, place % side
        odd = line % 2
        return line * side + step + odd * (side - 1 - 2 * step)

    spot = snake(chip)

    def chip_at(shift):
        return snake((spot + shift + n_c) % n_c) * CORES + core

    relayed = n_c == 4

    def own_piece(c):
        return basis.at[c] if c < pairs else own_amps.at[c - pairs]

    def row_piece(d, c):
        return row_bases.at[d, c] if c < pairs else row_amps.at[c - pairs, d]

    def col_piece(k, c):
        return col_bases.at[k, c] if c < pairs else col_amps.at[c - pairs, k]

    def remote(src, dst, send, recv, device):
        return pltpu.make_async_remote_copy(
            src_ref=src,
            dst_ref=dst,
            send_sem=send,
            recv_sem=recv,
            device_id=device,
            device_id_type=pl.DeviceIdType.MESH,
        )

    def plane(r, c):
        return remote(
            own_piece(c),
            row_piece(me, c),
            plane_send.at[r, c],
            plane_recv.at[r, c],
            (z, chip_at(r)),
        )

    def corner(c):
        way = 1 if c % 2 == 0 else -1
        d = chip_at(-way)
        return remote(
            row_piece(d, c),
            row_piece(d, c),
            plane_send.at[2, c],
            plane_recv.at[2, c],
            (z, chip_at(way)),
        )

    def is_corner(r, c):
        return relayed and r == 2 and c < pairs

    def plane_in(r, c):
        d = chip_at(-r)
        return remote(
            row_piece(d, c), row_piece(d, c), plane_send.at[r, c], plane_recv.at[r, c], (z, d)
        )

    def to_mate(r, c):
        d = chip_at(-r)
        src = own_piece(c) if r == 0 else row_piece(d, c)
        return remote(src, row_piece(d, c), mate_send.at[r, c], mate_recv.at[r, c], (z, mate))

    def mate_source(r):
        return snake((spot - r + n_c) % n_c) * CORES + (CORES - 1 - core)

    def mate_in(r, c):
        d = mate_source(r)
        return remote(
            row_piece(d, c), row_piece(d, c), mate_send.at[r, c], mate_recv.at[r, c], (z, mate)
        )

    def direct(c):
        return c >= pairs

    def parts(c):
        return range(SPLIT if c < pairs else 1)

    def part(ref, c, h):
        rows = size // SPLIT
        return ref.at[pl.ds(h * rows, rows)] if c < pairs else ref

    def lift(t, c, sign, h):
        alone = direct(c) or t == 1
        k = z if alone else z - sign * (t - 1)
        src = own_piece(c) if alone else col_piece(k, c)
        send, recv = (up_send, up_recv) if sign > 0 else (down_send, down_recv)
        slot = c * SPLIT + h
        return remote(
            part(src, c, h),
            part(col_piece(k, c), c, h),
            send.at[t, slot],
            recv.at[t, slot],
            (z + sign * (t if direct(c) else 1), me),
        )

    def lift_in(t, c, sign, h):
        k = z - sign * t
        send, recv = (up_send, up_recv) if sign > 0 else (down_send, down_recv)
        slot = c * SPLIT + h
        block = part(col_piece(k, c), c, h)
        return remote(block, block, send.at[t, slot], recv.at[t, slot], (z - sign, me))

    def place(sign):
        return z if sign > 0 else n_i - 1 - z

    def is_main(c, sign):
        return (c % 2 == 0) == (sign > 0)

    def both(a, b):
        return jnp.logical_and(a, b)

    def moves(t, c, sign):
        at = place(sign)
        if direct(c):
            return at <= n_i - 1 - t
        if c >= pairs or (t > 1 and is_main(c, sign)):
            return both(at >= t - 1, at <= n_i - 2)
        if t > 1:
            return None
        return at <= n_i - 3 if is_main(c, sign) else at == 0

    def comes(t, c, sign):
        at = place(sign)
        if c >= pairs or (t > 1 and is_main(c, sign)):
            return at >= t
        if t > 1:
            return None
        return both(at >= 1, at <= n_i - 2) if is_main(c, sign) else at == 1

    def returns(t, c, sign):
        at = place(sign)
        if t == 1:
            return at <= n_i - 3 if is_main(c, sign) else at == 0
        return at <= n_i - 1 - t if is_main(c, sign) else None

    def when(condition, action):
        if condition is not None:
            pl.when(condition)(action)

    def give_back(t, c, sign):
        k = z - sign * t
        spot_of = t + (0 if sign > 0 else n_i)
        return remote(
            back_out.at[k, c],
            back_in.at[z, c],
            back_send.at[spot_of, c],
            back_recv.at[spot_of, c],
            (k, me),
        )

    def take_back(t, c, sign):
        k = z + sign * t
        spot_of = t + (0 if sign > 0 else n_i)
        return remote(
            back_out.at[k, c],
            back_in.at[k, c],
            back_send.at[spot_of, c],
            back_recv.at[spot_of, c],
            (k, me),
        )

    def send_own(c):
        for t in reversed(range(1, n_i if direct(c) else 2)):
            for sign in (1, -1):
                for h in parts(c):
                    when(moves(t, c, sign), lambda: lift(t, c, sign, h).start())
        for r in range(1, n_c):
            if not is_corner(r, c):
                plane(r, c).start()
        to_mate(0, c).start()

    def pass_column(t, c):
        for h in parts(c):
            for sign in (1, -1):
                arrives = comes(t, c, sign)
                when(arrives, lambda: lift_in(t, c, sign, h).wait_recv())
                onward = moves(t + 1, c, sign) if t + 1 < n_i and not direct(c) else None
                if arrives is not None and onward is not None:
                    when(both(arrives, onward), lambda: lift(t + 1, c, sign, h).start())

    def pass_row(r, c):
        plane_in(r, c).wait_recv()
        if relayed and c < pairs and r == (1 if c % 2 == 0 else n_c - 1):
            corner(c).start()
        to_mate(r, c).start()

    near = [r for r in range(1, n_c) if not is_corner(r, 0)]
    near = near + [r for r in range(1, n_c) if is_corner(r, 0)]

    barrier = pltpu.get_barrier_semaphore()

    def greet(device):
        pl.semaphore_signal(
            barrier, inc=1, device_id=device, device_id_type=pl.DeviceIdType.MESH
        )

    greet((z, mate))
    for r in range(1, n_c):
        greet((z, chip_at(r)))
    for shift in range(1, n_i):
        greet(((z + shift) % n_i, me))
    pl.semaphore_wait(barrier, n_c + n_i - 1)

    for c in range(pairs):
        send_own(c)

    for p in range(pairs):
        own_amps[0, p] = amplitudes[p].astype(jnp.bfloat16)
        basis_t[p] = basis[p].astype(jnp.float32).T.astype(jnp.bfloat16)
        entries = domain[z, pl.ds(me * pairs + p, 1), :]
        own_dom[p] = jnp.broadcast_to(entries, (width, size)).T

    for p in range(pairs):
        slots = column_nbr.shape[1]
        names = lax.broadcasted_iota(jnp.int32, (n_j, slots), 0)
        order = lax.broadcasted_iota(jnp.int32, (n_j, slots), 1)
        hit = jnp.logical_and(column_nbr[p : p + 1, :] == names, order < column_cnt[0, p])
        chosen = jnp.sum(jnp.where(hit, 1.0, 0.0), axis=1, keepdims=True)
        diagonal = lax.broadcasted_iota(jnp.int32, (n_j, n_j), 0) == lax.broadcasted_iota(
            jnp.int32, (n_j, n_j), 1
        )
        table = jnp.sum(
            jnp.where(diagonal, coupling_columns[p : p + 1, :], 0.0), axis=1, keepdims=True
        )
        weight[p, 0:n_j, :] = jnp.broadcast_to(chosen * table, (n_j, width))
        slots = row_nbr.shape[1]
        names = lax.broadcasted_iota(jnp.int32, (n_i, slots), 0)
        order = lax.broadcasted_iota(jnp.int32, (n_i, slots), 1)
        hit = jnp.logical_and(row_nbr[p : p + 1, :] == names, order < row_cnt[0, p])
        chosen = jnp.sum(jnp.where(hit, 1.0, 0.0), axis=1, keepdims=True)
        diagonal = lax.broadcasted_iota(jnp.int32, (n_i, n_i), 0) == lax.broadcasted_iota(
            jnp.int32, (n_i, n_i), 1
        )
        table = jnp.sum(
            jnp.where(diagonal, coupling_rows[...], 0.0), axis=1, keepdims=True
        )
        weight[p, n_j : n_j + n_i, :] = jnp.broadcast_to(chosen * table, (n_i, width))

    def picked(p, entries):
        own = jnp.concatenate([own_dom[p]] * (size // width), axis=1)
        match = jnp.where(own == entries, 1.0, 0.0).astype(jnp.bfloat16)
        return jnp.dot(basis_t[p], match, preferred_element_type=jnp.float32).astype(
            jnp.bfloat16
        )

    def pick_row(q, carry):
        entries = domain[z, pl.ds(q, 1), :]
        for p in range(pairs):
            row_pick[q, p * width : (p + 1) * width, :] = picked(p, entries)
        return carry

    def pick_col(k, carry):
        for p in range(pairs):
            entries = domain[k, pl.ds(me * pairs + p, 1), :]
            col_pick[k, p * width : (p + 1) * width, :] = picked(p, entries)
        return carry

    def lanes(q):
        return pl.ds(pl.multiple_of(q * width, width), width)

    def intersect_row(d, c, bases):
        q = d * pairs + c
        found = jnp.dot(row_pick[q], bases, preferred_element_type=jnp.float32)
        inter[:, lanes(q)] = found.astype(jnp.bfloat16)

    def intersect_col(k, c):
        rows = slice(c * width, (c + 1) * width)
        found = jnp.dot(
            col_pick[k, rows, :], col_bases[k, c], preferred_element_type=jnp.float32
        )
        inter[rows, lanes(n_j + k)] = found.astype(jnp.bfloat16)
        back_out[k, c] = found.astype(jnp.bfloat16)

    def meet_column(t, c):
        for sign in (1, -1):
            when(comes(t, c, sign), lambda: intersect_col(z - sign * t, c))

    def return_column(t, c):
        for sign in (1, -1):
            when(comes(t, c, sign), lambda: give_back(t, c, sign).start())

    def accept_column(t, c):
        rows = slice(c * width, (c + 1) * width)
        for sign in (1, -1):

            def accept():
                take_back(t, c, sign).wait_recv()
                k = z + sign * t
                turned = back_in[k, c].astype(jnp.float32).T
                inter[rows, lanes(n_j + k)] = turned.astype(jnp.bfloat16)

            when(returns(t, c, sign), accept)

    share = n_j // 4
    lax.fori_loop(0, n_i, pick_col, 0)
    send_own(pairs)
    for c in range(pairs):
        pass_column(1, c)
        for r in near:
            if not is_corner(r, c):
                pass_row(r, c)
        meet_column(1, c)
        lax.fori_loop(c * share, (c + 1) * share, pick_row, 0)
        return_column(1, c)
    pass_column(1, pairs)
    zero = jnp.zeros((pairs * width, width), jnp.bfloat16)
    inter[:, lanes(n_j + z)] = zero
    half[:, lanes(n_j + z)] = zero
    for c in range(pairs):
        for r in near:
            if is_corner(r, c):
                pass_row(r, c)
    for t in range(2, n_i):
        for c in range(pairs):
            pass_column(t, c)
            meet_column(t, c)
        if t == 2:
            for r in range(1, n_c):
                pass_row(r, pairs)
            lax.fori_loop(pairs * share, n_j, pick_row, 0)
            for c in range(pairs):
                return_column(t, c)
            for c in range(pairs):
                intersect_row(me, c, basis[c])
        else:
            for c in range(pairs):
                return_column(t, c)
        pass_column(t, pairs)
    for r in near:
        for c in range(pairs):
            d = chip_at(-r)
            intersect_row(d, c, row_bases[d, c])
    for r in range(n_c):
        for c in range(pairs):
            d = mate_source(r)
            mate_in(r, c).wait_recv()
            intersect_row(d, c, row_bases[d, c])
        mate_in(r, pairs).wait_recv()
    for t in range(1, n_i):
        for c in range(pairs):
            accept_column(t, c)

    def halve_row(it, d, amps):
        for c in range(pairs):
            q = d * pairs + c
            pair = jnp.dot(inter[:, lanes(q)], amps[c], preferred_element_type=jnp.float32)
            for p in range(pairs):
                rows = slice(p * width, (p + 1) * width)
                half[rows, lanes(q)] = (pair[rows] * weight[p, pl.ds(q, 1), :]).astype(
                    jnp.bfloat16
                )

    def halve_col(it, k):
        for p in range(pairs):
            rows = slice(p * width, (p + 1) * width)
            one = jnp.dot(
                inter[rows, lanes(n_j + k)],
                col_amps[it, k, p],
                preferred_element_type=jnp.float32,
            )
            half[rows, lanes(n_j + k)] = (one * weight[p, pl.ds(n_j + k, 1), :]).astype(
                jnp.bfloat16
            )

    for it in range(ITERS):
        c = pairs + it
        if it > 0:
            send_own(c)
        halve_row(it, me, own_amps.at[it])
        if it > 0:
            for r in range(1, n_c):
                pass_row(r, c)
        for r in range(1, n_c):
            d = chip_at(-r)
            halve_row(it, d, row_amps.at[it, d])
        for r in range(n_c):
            if it > 0:
                mate_in(r, c).wait_recv()
            d = mate_source(r)
            halve_row(it, d, row_amps.at[it, d])
        for t in range(1, n_i):
            if it > 0:
                pass_column(t, c)
            for sign in (1, -1):
                when(comes(t, c, sign), lambda: halve_col(it, z - sign * t))
        for p in range(pairs):
            rows = slice(p * width, (p + 1) * width)
            coupled = lax.dot_general(
                half[rows, :],
                inter[rows, :],
                (((1,), (1,)), ((), ())),
                preferred_element_type=jnp.float32,
            )
            across = jnp.broadcast_to(energy[p : p + 1, :], (width, width))
            gap = across.T + across - row_energy[0] - column_energy[p]
            current = amplitudes[p] if it == 0 else out[p]
            residual = exchange[p] + gap * current - coupled
            current = current - residual / (gap + level_shift)
            out[p] = current
            if it + 1 < ITERS:
                own_amps[it + 1, p] = current.astype(jnp.bfloat16)
            else:
                terms = exchange[p] * (2.0 * current - current.T)
                pair_out[:, p : p + 1] = jnp.sum(
                    jnp.sum(terms, axis=0, keepdims=True), axis=1, keepdims=True
                )

    for c in range(chunks):
        for r in range(1, n_c):
            (corner(c) if is_corner(r, c) else plane(r, c)).wait_send()
        for r in range(n_c):
            to_mate(r, c).wait_send()
        for sign in (1, -1):
            for t in range(1, n_i):
                for h in parts(c):
                    when(moves(t, c, sign), lambda: lift(t, c, sign, h).wait_send())
                if c < pairs:
                    when(comes(t, c, sign), lambda: give_back(t, c, sign).wait_send())


def local(
    n_i,
    n_d,
    pno_basis,
    domain_map,
    amplitudes,
    exchange_ints,
    pno_energy,
    row_energy,
    column_energy,
    coupling_rows,
    coupling_columns,
    row_neighbours,
    column_neighbours,
    row_counts,
    column_counts,
):
    _, pairs, size, width = pno_basis.shape
    n_j = n_d * pairs
    n_c = n_d // CORES
    chunks = pairs + ITERS
    vmem = pl.BlockSpec(memory_space=pltpu.VMEM)
    smem = pl.BlockSpec(memory_space=pltpu.SMEM)
    bf16 = jnp.bfloat16
    dma = pltpu.SemaphoreType.DMA
    new, pair_energy = pl.pallas_call(
        functools.partial(kernel, n_i, n_d),
        out_shape=(
            jax.ShapeDtypeStruct((pairs, width, width), jnp.float32),
            jax.ShapeDtypeStruct((1, pairs), jnp.float32),
        ),
        in_specs=[vmem] * 5 + [smem] * 2 + [vmem] * 4 + [smem] * 2,
        out_specs=(vmem, vmem),
        scratch_shapes=[
            pltpu.VMEM((n_d, pairs, size, width), bf16),
            pltpu.VMEM((n_i, pairs, size, width), bf16),
            pltpu.VMEM((ITERS, n_d, pairs, width, width), bf16),
            pltpu.VMEM((ITERS, n_i, pairs, width, width), bf16),
            pltpu.VMEM((ITERS, pairs, width, width), bf16),
            pltpu.VMEM((pairs, width, size), bf16),
            pltpu.VMEM((pairs, size, width), jnp.int32),
            pltpu.VMEM((n_j, pairs * width, size), bf16),
            pltpu.VMEM((n_i, pairs * width, size), bf16),
            pltpu.VMEM((pairs * width, (n_j + n_i) * width), bf16),
            pltpu.VMEM((pairs * width, (n_j + n_i) * width), bf16),
            pltpu.VMEM((pairs, n_j + n_i, width), jnp.float32),
            pltpu.VMEM((n_i, pairs, width, width), bf16),
            pltpu.VMEM((n_i, pairs, width, width), bf16),
            dma((n_c, chunks)),
            dma((n_c, chunks)),
            dma((n_c, chunks)),
            dma((n_c, chunks)),
            dma((n_i, chunks * SPLIT)),
            dma((n_i, chunks * SPLIT)),
            dma((n_i, chunks * SPLIT)),
            dma((n_i, chunks * SPLIT)),
            dma((2 * n_i, pairs)),
            dma((2 * n_i, pairs)),
        ],
        compiler_params=pltpu.CompilerParams(collective_id=0, has_side_effects=True),
        name="cepa",
    )(
        pno_basis[0],
        domain_map,
        amplitudes[0],
        exchange_ints[0],
        pno_energy[0],
        row_energy,
        column_energy,
        coupling_rows,
        coupling_columns.T,
        row_neighbours[0],
        column_neighbours[0],
        row_counts,
        column_counts,
    )
    return new[None], pair_energy


def solution(mesh):
    in_specs = (
        P("ia", "ja", None, None),
        P(),
        P("ia", "ja", None, None),
        P("ia", "ja", None, None),
        P("ia", "ja", None),
        P("ia"),
        P("ja"),
        P("ia", None),
        P(None, "ja"),
        P("ia", "ja", None),
        P("ia", "ja", None),
        P("ia", "ja"),
        P("ia", "ja"),
    )
    out_specs = (P("ia", "ja", None, None), P("ia", "ja"))
    body = functools.partial(local, mesh.shape["ia"], mesh.shape["ja"])
    return jax.shard_map(body, mesh=mesh, in_specs=in_specs, out_specs=out_specs, check_vma=False)
```
